32 devices in a mesh: blk: 8 (over y, x, core), mod: 4 (over z).
Axes of the slice: x: 2, y: 2, z: 4, core: 2. Of those that a mesh axis runs over, the one named last changes fastest.
Arguments:
- act: bfloat16 [4, 32, 8192], P('mod', None, 'blk'), may hold values from -6 to 6
- grad: bfloat16 [4, 64, 8192], P('mod', None, 'blk'), may hold values from -40 to 40
- train: bfloat16 [4, 16384, 2048], P('mod', 'blk'), may hold values from -24 to 24
- pre_out: float32 [4, 64, 64], P('mod'), may hold values from -0.75 to 0.75
- pre_in: float32 [4, 32, 32], P('mod'), may hold values from -1 to 1
- doc_ids: int32 [8192, 1], P('blk'), may hold values from 0 to 255; in each aligned block of 1024 rows (0 to 1023, 1024 to 2047, ...) at most 4 rows name the same one
- owners: int32 [256], replicated, may hold values from 0 to 255, each once
Outputs:
- scores: float32 [4, 256, 16384], P('mod', None, 'blk')
The draws below stay inside these ranges and needn't reach their ends.
Inputs may be any that keep to these rules, and one draw needn't show every extreme that they name: `doc_ids`: among the 1024 tokens of one index of blk no document has more than 4 tokens, and some document has exactly 4 in some such block; every document has at least one token. `owners`: A permutation of the 256 documents.
All inputs are finite; a program needn't handle non-finite values.
Results may differ from the reference program's by a relative error of at most 0.0029.
Values may be sent and summed in bfloat16 or wider, within the bound.
A program may use at most 64 MiB of HBM per device.

```python
import math
import jax
import jax.numpy as jnp
import numpy as np
from jax import lax

A = 32
G = 64
MOST = 4
TOK_DEV = 1024
MODULES = 4
DOCS = 256
QTOK = 8192
TRAIN = 16384
N_BLK = 8


def draw_grad(key, part):
    token_key = jax.random.fold_in(jax.random.fold_in(key, 7), 1)
    value_key = jax.random.fold_in(jax.random.fold_in(key, 7), 2)
    level = jnp.arange(MODULES, dtype=jnp.float32) / max(MODULES - 1, 1)
    token_scale = jnp.exp(jax.random.uniform(token_key, (QTOK,), jnp.float32, jnp.log(0.3), jnp.log(3.0)))
    values = jnp.clip(jax.random.normal(value_key, (MODULES, G, QTOK), jnp.float32), -4.0, 4.0)
    module_scale = 3.0 ** level
    return (values * module_scale[:, None, None] * token_scale[None, None, :]).astype(jnp.bfloat16)


def block_scale(stream_key, extent, pieces, least, high):
    level = 1.0
    for axis_at, parts in pieces:
        steps = jax.random.uniform(jax.random.fold_in(jax.random.fold_in(stream_key, 6), axis_at), (parts,), jnp.float32, least / len(pieces), high / len(pieces))
        level = level * jnp.repeat(jnp.exp(steps), extent[axis_at] // parts).reshape((-1,) + (1,) * (len(extent) - 1 - axis_at))
    return level


def deal_out(rng, own, number, rows, number_of, top, bound, skew):
    sequence = jax.random.permutation(rng, number_of)
    crowded, usual = portions_of(number_of, rows * top, bound, skew, True), portions_of(number_of, rows * top, bound, skew, False)
    places = jnp.arange(number_of)

    def named(lengths, turn):
        used = int((lengths > 0).sum())
        fixed = max(1, used // 4)
        moved = fixed + (places - fixed + turn * (used - fixed)) % max(1, number_of - fixed)
        return jnp.zeros((number_of,), jnp.int32).at[sequence[jnp.where(places < fixed, places, moved)]].set(jnp.asarray(lengths, jnp.int32))

    lengths = jnp.where(number % 4 == 0, named(crowded, number // 4), named(usual, number - number // 4 - 1))
    mixed = jax.random.permutation(jax.random.fold_in(own, 3), number_of)
    source_of, taker = mixed[0:number_of // 2 * 2:2], mixed[1:number_of // 2 * 2:2]
    room = jnp.minimum(lengths[source_of] - 1, bound - lengths[taker]) // 2
    room = jnp.where((source_of == sequence[0]) | (taker == sequence[0]) | (lengths[taker] == 0), 0, jnp.maximum(room, 0))
    moved = jax.random.randint(jax.random.fold_in(own, 4), (number_of // 2,), 0, 1 << 20) % (room + 1)
    lengths = lengths.at[source_of].add(-moved).at[taker].add(moved)
    labels = jnp.searchsorted(jnp.cumsum(lengths), jnp.arange(rows * top), side="right").astype(jnp.int32)
    table = labels.reshape(top, rows).T
    table = table[jax.random.permutation(jax.random.fold_in(own, 1), rows)]
    turn = jax.random.randint(jax.random.fold_in(own, 2), (rows, 1), 0, top)
    return jnp.take_along_axis(table, (jnp.arange(top)[None, :] + turn) % top, axis=1)


def portions_of(count, total, most, skew, full):
    weights = [(1 << 20) // math.isqrt(standing ** skew) + 1 for standing in range(1, count + 1)]
    largest = most if full else min(most, max(-(-total // count), total * weights[0] // sum(weights)))
    least = 1 if total - largest >= count - 1 else 0
    given, spare = [largest] + [least] * (count - 1), total - largest - least * (count - 1)
    while spare > 0:
        free = [i for i in range(1, count) if given[i] < largest] or [i for i in range(1, count) if given[i] < most]
        pool, left = sum([weights[i] for i in free]), spare
        for i in free:
            addition = min(most - given[i], max(1, left * weights[i] // pool), spare)
            given[i] = given[i] + addition
            spare = spare - addition
    return np.array(given)


def noise(key, extent, spread, most, pieces=(), kind=jnp.bfloat16):
    result = jax.random.normal(key, extent, jnp.float32) * spread
    if len(pieces) > 0:
        result = block_scale(key, extent, pieces, -0.22, 0.18) * result
    return jnp.clip(result, min=-most, max=most).astype(kind)


def setup_inputs(seed: int = 0) -> dict:
    seeds = jax.random.split(jax.random.key(seed), 8)
    act = noise(seeds[0], (MODULES, A, QTOK), 1.0, 6.0, ((0, 4), (2, 8)))
    grad = draw_grad(jax.random.fold_in(seeds[7], 71), 0)
    train = noise(seeds[2], (MODULES, TRAIN, G * A), 4.0, 24.0, ((0, 4), (1, 8)))
    pre_out = noise(seeds[3], (MODULES, G, G), G ** -0.5, 0.75, ((0, 4),), jnp.float32)
    pre_in = noise(seeds[4], (MODULES, A, A), A ** -0.5, 1.0, ((0, 4),), jnp.float32)
    doc_ids_keys = jax.random.split(jax.random.fold_in(seeds[5], 1), QTOK // TOK_DEV)
    doc_ids_turns = jax.random.permutation(jax.random.fold_in(seeds[5], 3), QTOK // TOK_DEV)
    doc_ids = jax.vmap(lambda own, number: deal_out(jax.random.fold_in(seeds[5], 2), own, number, TOK_DEV, DOCS, 1, MOST, 2))(doc_ids_keys, doc_ids_turns).reshape((QTOK, 1))
    owners = jax.random.permutation(seeds[6], DOCS).astype(jnp.int32)
    return dict(act=act, grad=grad, train=train, pre_out=pre_out, pre_in=pre_in, doc_ids=doc_ids, owners=owners)


def reference(act, grad, train, pre_out, pre_in, doc_ids, owners):
    doc_index = doc_ids[:, 0]
    onehot = (doc_index[:, None] == jnp.arange(DOCS, dtype=jnp.int32)[None, :]).astype(jnp.float32)

    def per_module(module):
        act_rows = act[module].astype(jnp.float32)
        grad_rows = grad[module].astype(jnp.float32)

        def step(total, block):
            act_block = lax.dynamic_slice_in_dim(act_rows, block * TOK_DEV, TOK_DEV, 1)
            grad_block = lax.dynamic_slice_in_dim(grad_rows, block * TOK_DEV, TOK_DEV, 1)
            hot_block = lax.dynamic_slice_in_dim(onehot, block * TOK_DEV, TOK_DEV, 0)
            outer = (grad_block[:, None, :] * act_block[None, :, :]).reshape(G * A, TOK_DEV)
            return (total + jnp.dot(outer, hot_block, precision=lax.Precision.HIGHEST), None)
        total, _ = lax.scan(step, jnp.zeros((G * A, DOCS), jnp.float32), jnp.arange(N_BLK, dtype=jnp.int32))
        doc_grad = total.T.reshape(DOCS, G, A)
        left = jnp.einsum('hg,dga->dha', pre_out[module], doc_grad, precision=lax.Precision.HIGHEST)
        return jnp.einsum('dha,ab->dhb', left, pre_in[module], precision=lax.Precision.HIGHEST)
    cond = lax.map(per_module, jnp.arange(MODULES, dtype=jnp.int32))
    squares = lax.optimization_barrier(jnp.sum(cond * cond, axis=(0, 2, 3)))
    inv_norm = 1.0 / jnp.sqrt(squares + 1e-06)
    ordered = cond[:, owners] * inv_norm[owners][None, :, None, None]
    doc_b = ordered.reshape(MODULES, DOCS, G * A).astype(jnp.bfloat16)

    def score_module(module):
        return lax.dot_general(doc_b[module], train[module], (((1,), (1,)), ((), ())), preferred_element_type=jnp.float32)
    return lax.map(score_module, jnp.arange(MODULES, dtype=jnp.int32))
```

```python
import functools

import jax
import jax.numpy as jnp
from jax import lax
from jax.experimental import pallas as pl
from jax.experimental.pallas import tpu as pltpu
from jax.sharding import PartitionSpec as P

MOST = 4
LANES = 128
WIDE = 256
CHUNKS = 4
UNROLL = 8
NT = (((1,), (1,)), ((), ()))
TN = (((0,), (0,)), ((), ()))
HIGH = lax.Precision.HIGHEST


def kernel(
    blocks, mods,
    ids_hbm, own_hbm, act_hbm, grad_hbm, pre_out_hbm, pre_in_hbm, train_ref,
    acc, norms,
    ids_ref, own_ref, act_ref, grad_ref, pre_out_ref, pre_in_ref, train_v, send, recv, kin, lay, gath, sq_out, sq_in, tot,
    t_sem, i_sem, go, sa, ra, sg, rg, sp, rp, sn, rn, st, rt,
):
    a_dim, tokens = act_hbm.shape
    g_dim = grad_hbm.shape[0]
    docs = own_hbm.shape[1]
    per = docs // blocks
    slots = per * MOST
    chips = blocks // 2
    feats = a_dim * g_dim
    part = feats // CHUNKS
    rows_all = train_ref.shape[0]
    tiles = rows_all // WIDE
    packs = LANES // a_dim
    band = WIDE // a_dim
    groups = per // band
    steps = g_dim // packs

    blk = lax.axis_index("blk")
    mod = lax.axis_index("mod")
    chip = lax.div(blk, 2)
    core = lax.rem(blk, 2)
    mate = chip * 2 + (1 - core)

    loads = [
        pltpu.make_async_copy(
            train_ref.at[pl.ds(i * WIDE, WIDE)], train_v.at[pl.ds(i * WIDE, WIDE)], t_sem.at[i]
        )
        for i in range(tiles)
    ]
    small = [
        pltpu.make_async_copy(src, dst, i_sem.at[i])
        for i, (src, dst) in enumerate((
            (ids_hbm, ids_ref), (own_hbm, own_ref), (act_hbm, act_ref),
            (grad_hbm, grad_ref), (pre_out_hbm, pre_out_ref), (pre_in_hbm, pre_in_ref)))
    ]
    for load in small:
        load.start()
    barrier = pltpu.get_barrier_semaphore()
    for c in range(chips):
        @pl.when(c * 2 != blk)
        def _():
            pl.semaphore_signal(barrier, inc=1, device_id={"blk": c * 2}, device_id_type=pl.DeviceIdType.MESH)
    small[0].wait()
    small[1].wait()

    ids = ids_ref[...].astype(jnp.float32)
    own_t = jnp.transpose(jnp.broadcast_to(own_ref[...].astype(jnp.float32), (WIDE, docs)))
    before_t = (
        lax.broadcasted_iota(jnp.int32, (WIDE, WIDE), 0) < lax.broadcasted_iota(jnp.int32, (WIDE, WIDE), 1)
    ).astype(jnp.float32).astype(jnp.bfloat16)
    place = lax.broadcasted_iota(jnp.int32, (docs, WIDE), 0).astype(jnp.float32) * MOST
    carry = jnp.zeros((docs, 1), jnp.float32)
    slot_parts = []
    for t in range(tokens // WIDE):
        match = own_t == ids[:, t * WIDE:(t + 1) * WIDE]
        hot = jnp.where(match, 1.0, 0.0)
        before = jnp.dot(hot.astype(jnp.bfloat16), before_t, preferred_element_type=jnp.float32)
        slot_parts.append(jnp.sum(jnp.where(match, place + before + carry, 0.0), axis=0, keepdims=True))
        carry = carry + jnp.sum(hot, axis=1, keepdims=True)
    slot = jnp.concatenate(slot_parts, axis=1).astype(jnp.int32)
    small[2].wait()
    small[3].wait()
    token_rows = jnp.concatenate([act_ref[...], grad_ref[...]], axis=0)

    def a2a(c, k, dest, src):
        return pltpu.make_async_remote_copy(
            src_ref=send.at[c, k], dst_ref=recv.at[src], send_sem=sa.at[c, k],
            recv_sem=ra.at[c, core], device_id={"blk": dest}, device_id_type=pl.DeviceIdType.MESH)

    line = lax.broadcasted_iota(jnp.int32, (2 * slots, tokens), 0)
    sent = []
    for c in list(range(1, chips)) + [0]:
        to = lax.rem(chip + c, chips)
        hot = jnp.where(line == slot - to * (2 * slots), 1.0, 0.0).astype(jnp.bfloat16)
        packed = lax.dot_general(token_rows, hot, NT, preferred_element_type=jnp.float32).astype(jnp.bfloat16)
        halves = [packed[:, :slots], packed[:, slots:]]
        if c:
            for k in range(2):
                send[c, k] = halves[k]
                sent.append(a2a(c, k, to * 2 + k, blk))
        else:
            first = core == 0
            send[0, 0] = jnp.where(first, halves[1], halves[0])
            sent.append(a2a(0, 0, mate, blk))
            recv[blk] = jnp.where(first, halves[0], halves[1])


    @pl.when(core == 0)
    def _():
        pl.semaphore_wait(barrier, blocks - 1)
        pl.semaphore_signal(go, inc=1, device_id={"blk": mate}, device_id_type=pl.DeviceIdType.MESH)

    @pl.when(core == 1)
    def _():
        pl.semaphore_wait(go, 1)

    for copy in sent:
        copy.start()
    for load in loads:
        load.start()

    @pl.when(core == 1)
    def _():
        for d in range(1, mods):
            pl.semaphore_signal(barrier, inc=1, device_id={"mod": lax.rem(mod + d, mods)}, device_id_type=pl.DeviceIdType.MESH)


    row_w = lax.broadcasted_iota(jnp.int32, (WIDE, WIDE), 0)
    col_w = lax.broadcasted_iota(jnp.int32, (WIDE, WIDE), 1)
    small[4].wait()
    small[5].wait()
    tall = jnp.concatenate([pre_in_ref[...]] * band, axis=0)
    kin[...] = jnp.where(row_w // a_dim == col_w // a_dim, jnp.concatenate([tall] * band, axis=1), 0.0)
    left = jnp.concatenate([pre_out_ref[pl.ds(i, steps, stride=packs), :] for i in range(packs)], axis=0)
    spread = (
        lax.broadcasted_iota(jnp.int32, (a_dim, WIDE), 0) == lax.broadcasted_iota(jnp.int32, (a_dim, WIDE), 1) % a_dim
    ).astype(jnp.float32).astype(jnp.bfloat16)
    span = band * MOST
    slot_doc = (lax.broadcasted_iota(jnp.int32, (slots, WIDE), 0) % span) // MOST
    in_doc = (slot_doc == lax.broadcasted_iota(jnp.int32, (slots, WIDE), 1) // a_dim).astype(jnp.float32)
    slot_group = lax.broadcasted_iota(jnp.int32, (g_dim, slots), 1) // span
    in_group = [(slot_group == q).astype(jnp.float32).astype(jnp.bfloat16) for q in range(groups)]

    def wait_tokens(c, k):
        src = lax.rem(chip - c + chips, chips) * 2 + k
        pltpu.make_async_remote_copy(
            src_ref=send.at[0, 0], dst_ref=recv.at[src], send_sem=sa.at[0, 0],
            recv_sem=ra.at[c, k], device_id={"blk": src}, device_id_type=pl.DeviceIdType.MESH).wait_recv()

    wait_tokens(0, 1 - core)
    for c in range(1, chips):
        for k in range(2):
            wait_tokens(c, k)

    rights, lefts = [], []
    for s in range(blocks):
        wide = lax.dot_general(recv[s, :a_dim, :], spread, TN, preferred_element_type=jnp.float32)
        rights.append((wide * in_doc).astype(jnp.bfloat16))
        y = recv[s, a_dim:, :]
        lefts.append(jnp.concatenate([y * m for m in in_group], axis=0))
    doc_grad = jnp.dot(
        jnp.concatenate(lefts, axis=1), jnp.concatenate(rights, axis=0), preferred_element_type=jnp.float32)
    half = jnp.concatenate(
        [jnp.dot(left, doc_grad[q * g_dim:(q + 1) * g_dim], precision=HIGH, preferred_element_type=jnp.float32)
         for q in range(groups)], axis=0)
    cond = jnp.dot(half, kin[...], precision=HIGH, preferred_element_type=jnp.float32)

    rows = groups * steps
    lane_pack = lax.broadcasted_iota(jnp.int32, (rows, LANES), 1) // a_dim
    for side in range(WIDE // LANES):
        outs = [None] * packs
        for i in range(packs):
            x = jnp.concatenate(
                [cond[q * g_dim + i * steps:q * g_dim + (i + 1) * steps, side * LANES:(side + 1) * LANES]
                 for q in range(groups)], axis=0)
            for pos in range(packs):
                turn = ((i - pos) % packs) * a_dim
                moved = pltpu.roll(x, turn, 1) if turn else x
                outs[pos] = moved if outs[pos] is None else jnp.where(lane_pack == i, moved, outs[pos])
        for pos in range(packs):
            lay[pl.ds((side * packs + pos) * rows, rows), :] = outs[pos]

    def block_rows(b):
        return pl.ds(pl.multiple_of(b * per, per), per)

    def across(ch, c):
        mine = gath.at[ch, block_rows(blk)]
        return pltpu.make_async_remote_copy(
            src_ref=mine, dst_ref=mine, send_sem=sg.at[ch, c], recv_sem=rg.at[ch, c],
            device_id={"blk": lax.rem(chip + c, chips) * 2 + core}, device_id_type=pl.DeviceIdType.MESH)

    def came(ch, c):
        theirs = gath.at[ch, block_rows(lax.rem(chip - c + chips, chips) * 2 + core)]
        return pltpu.make_async_remote_copy(
            src_ref=theirs, dst_ref=theirs, send_sem=sg.at[ch, c], recv_sem=rg.at[ch, c],
            device_id={"blk": lax.rem(chip + c, chips) * 2 + core}, device_id_type=pl.DeviceIdType.MESH)

    def pass_on(ch, c, side):
        it = gath.at[ch, block_rows(lax.rem(chip - c + chips, chips) * 2 + side)]
        return pltpu.make_async_remote_copy(
            src_ref=it, dst_ref=it, send_sem=sp.at[ch, c], recv_sem=rp.at[ch, c],
            device_id={"blk": mate}, device_id_type=pl.DeviceIdType.MESH)

    squares = jnp.zeros((per, LANES), jnp.float32)
    per_chunk = part // LANES
    for ch in range(CHUNKS):
        for u in range(per_chunk):
            j = ch * per_chunk + u
            tile = jnp.concatenate(
                [lay[pl.ds(q * steps + j, band, stride=rows), :] for q in range(groups)], axis=0)
            squares = squares + tile * tile
            gath[ch, block_rows(blk), pl.ds(u * LANES, LANES)] = tile.astype(jnp.bfloat16)
        for c in range(1, chips):
            copy = across(ch, c)
            copy.start()
            sent.append(copy)
        copy = pass_on(ch, 0, core)
        copy.start()
        sent.append(copy)
    sq_out[...] = jnp.broadcast_to(jnp.sum(squares, axis=1, keepdims=True), (per, LANES))

    def square_copy(d):
        return pltpu.make_async_remote_copy(
            src_ref=sq_out, dst_ref=sq_in.at[d], send_sem=sn.at[d], recv_sem=rn.at[d],
            device_id={"mod": lax.rem(mod + d, mods)}, device_id_type=pl.DeviceIdType.MESH)

    def total_copy(d, src):
        return pltpu.make_async_remote_copy(
            src_ref=tot, dst_ref=norms.at[block_rows(src)], send_sem=st.at[d], recv_sem=rt.at[d],
            device_id={"blk": lax.rem(blk + d, blocks)}, device_id_type=pl.DeviceIdType.MESH)

    @pl.when(core == 1)
    def _():
        pl.semaphore_wait(barrier, mods - 1)
        pl.semaphore_signal(go, inc=1, device_id={"blk": mate}, device_id_type=pl.DeviceIdType.MESH)

    @pl.when(core == 0)
    def _():
        pl.semaphore_wait(go, 1)

    for d in range(1, mods):
        copy = square_copy(d)
        copy.start()
        sent.append(copy)

    def forward(ch):
        for c in range(1, chips):
            came(ch, c).wait_recv()
            copy = pass_on(ch, c, core)
            copy.start()
            sent.append(copy)

    def multiply(ch):
        for c in range(chips):
            pass_on(ch, c, 1 - core).wait_recv()
        if ch == 0:
            for load in loads:
                load.wait()

        @pl.loop(0, tiles, unroll=UNROLL)
        def _(i):
            at = pl.ds(pl.multiple_of(i * WIDE, WIDE), WIDE)
            product = lax.dot_general(
                gath[ch], train_v[at, ch * part:(ch + 1) * part], NT, preferred_element_type=jnp.float32)
            if ch == 0:
                acc[:, at] = product
            else:
                acc[:, at] = acc[:, at] + product

    forward(0)
    for ch in range(CHUNKS):
        if ch + 1 < CHUNKS:
            forward(ch + 1)
        if ch == 2:
            for d in range(1, mods):
                square_copy(d).wait_recv()
            total = sq_out[...]
            for d in range(1, mods):
                total = total + sq_in[d]
            tot[...] = total
            norms[block_rows(blk), :] = total
            for d in range(1, blocks):
                copy = total_copy(d, blk)
                copy.start()
                sent.append(copy)
        multiply(ch)
    for d in range(1, blocks):
        total_copy(d, lax.rem(blk - d + blocks, blocks)).wait_recv()
    for copy in sent:
        copy.wait_send()


def body(blocks, mods, act, grad, train, pre_out, pre_in, doc_ids, owners):
    a_dim, tokens = act.shape[1:]
    g_dim = grad.shape[1]
    docs = owners.shape[0]
    per = docs // blocks
    chips = blocks // 2
    feats = a_dim * g_dim
    part = feats // CHUNKS
    rows = train.shape[1]
    tiles = rows // WIDE
    slots = per * MOST
    band = WIDE // a_dim
    vmem = pl.BlockSpec(memory_space=pltpu.VMEM)
    hbm = pl.BlockSpec(memory_space=pltpu.HBM)
    dma = pltpu.SemaphoreType.DMA
    raw, norms = pl.pallas_call(
        functools.partial(kernel, blocks, mods),
        out_shape=(
            pltpu.VMEM((docs, rows), jnp.float32),
            pltpu.VMEM((docs, LANES), jnp.float32),
        ),
        in_specs=[hbm] * 7,
        out_specs=(vmem, vmem),
        scratch_shapes=[
            pltpu.VMEM((1, tokens), jnp.int32),
            pltpu.VMEM((1, docs), jnp.int32),
            pltpu.VMEM((a_dim, tokens), jnp.bfloat16),
            pltpu.VMEM((g_dim, tokens), jnp.bfloat16),
            pltpu.VMEM((g_dim, g_dim), jnp.float32),
            pltpu.VMEM((a_dim, a_dim), jnp.float32),
            pltpu.VMEM((rows, feats), jnp.bfloat16),
            pltpu.VMEM((chips, 2, a_dim + g_dim, slots), jnp.bfloat16),
            pltpu.VMEM((blocks, a_dim + g_dim, slots), jnp.bfloat16),
            pltpu.VMEM((WIDE, WIDE), jnp.float32),
            pltpu.VMEM((per * g_dim * a_dim // LANES, LANES), jnp.float32),
            pltpu.VMEM((CHUNKS, docs, part), jnp.bfloat16),
            pltpu.VMEM((per, LANES), jnp.float32),
            pltpu.VMEM((mods, per, LANES), jnp.float32),
            pltpu.VMEM((per, LANES), jnp.float32),
            dma((tiles,)), dma((6,)), pltpu.SemaphoreType.REGULAR,
            dma((chips, 2)), dma((chips, 2)),
            dma((CHUNKS, chips)), dma((CHUNKS, chips)),
            dma((CHUNKS, chips)), dma((CHUNKS, chips)),
            dma((mods,)), dma((mods,)),
            dma((blocks,)), dma((blocks,)),
        ],
        compiler_params=pltpu.CompilerParams(
            collective_id=0, has_side_effects=True, vmem_limit_bytes=48 * 1024 * 1024),
    )(*[pltpu.with_memory_space_constraint(x, pltpu.HBM) for x in (
        doc_ids.reshape(1, tokens), owners.reshape(1, docs), act[0], grad[0], pre_out[0], pre_in[0], train[0])])
    return (raw * (1.0 / jnp.sqrt(norms[:, :1] + 1e-06)))[None]


def solution(mesh):
    blocks, mods = mesh.shape["blk"], mesh.shape["mod"]
    return jax.shard_map(
        functools.partial(body, blocks, mods),
        mesh=mesh,
        in_specs=(
            P("mod", None, "blk"),
            P("mod", None, "blk"),
            P("mod", "blk", None),
            P("mod", None, None),
            P("mod", None, None),
            P("blk", None),
            P(),
        ),
        out_specs=P("mod", None, "blk"),
        check_vma=False,
    )
```

```python
import functools

import jax
import jax.numpy as jnp
from jax import lax
from jax.experimental import pallas as pl
from jax.experimental.pallas import tpu as pltpu
from jax.sharding import PartitionSpec as P

MOST = 4
LANES = 128
WIDE = 256
CHUNKS = 4
UNROLL = 8
NT = (((1,), (1,)), ((), ()))
TN = (((0,), (0,)), ((), ()))
HIGH = lax.Precision.HIGHEST


def kernel(
    blocks, mods,
    ids_hbm, own_hbm, act_hbm, grad_hbm, pre_out_hbm, pre_in_hbm, train_ref,
    acc, norms, inv, kout, ids_ref, own_ref, act_ref, grad_ref, pre_out_ref, pre_in_ref, train_v, send, recv, kin, lay, gath, sq_out, sq_in, tot,
    t_sem, i_sem, go, sa, ra, sg, rg, rp, sn, rn, st, rt,
):
    a_dim, tokens = act_hbm.shape
    g_dim = grad_hbm.shape[0]
    docs = own_hbm.shape[1]
    per = docs // blocks
    slots = per * MOST
    chips = blocks // 2
    feats = a_dim * g_dim
    part = feats // CHUNKS
    rows_all = train_ref.shape[0]
    tiles = rows_all // WIDE
    packs = LANES // a_dim
    band = WIDE // a_dim
    groups = per // band
    steps = g_dim // packs

    blk = lax.axis_index("blk")
    mod = lax.axis_index("mod")
    chip = lax.div(blk, 2)
    core = lax.rem(blk, 2)
    mate = chip * 2 + (1 - core)
    square = chips == 4
    if square:
        hops = [chip, chip + 1 - 2 * lax.rem(chip, 2), lax.rem(chip + 2, chips), chips - 1 - chip]

    def onto(c):
        return hops[c] if square else lax.rem(chip + c, chips)

    def source(c):
        return hops[c] if square else lax.rem(chip - c + chips, chips)

    order = list(range(chips - 1, 0, -1))

    loads = [
        pltpu.make_async_copy(
            train_ref.at[pl.ds(i * WIDE, WIDE)], train_v.at[pl.ds(i * WIDE, WIDE)], t_sem
        )
        for i in range(tiles)
    ]
    small = [
        pltpu.make_async_copy(src, dst, i_sem.at[i])
        for i, (src, dst) in enumerate((
            (ids_hbm, ids_ref), (own_hbm, own_ref), (act_hbm, act_ref),
            (grad_hbm, grad_ref), (pre_out_hbm, pre_out_ref), (pre_in_hbm, pre_in_ref)))
    ]
    for load in small:
        load.start()
    barrier = pltpu.get_barrier_semaphore()
    for c in range(chips):
        @pl.when(c * 2 != blk)
        def _():
            pl.semaphore_signal(barrier, inc=1, device_id={"blk": c * 2}, device_id_type=pl.DeviceIdType.MESH)
    small[0].wait()
    small[1].wait()

    ids = ids_ref[...].astype(jnp.float32)
    own_t = jnp.transpose(jnp.broadcast_to(own_ref[...].astype(jnp.float32), (WIDE, docs)))
    before_t = (
        lax.broadcasted_iota(jnp.int32, (WIDE, WIDE), 0) < lax.broadcasted_iota(jnp.int32, (WIDE, WIDE), 1)
    ).astype(jnp.float32).astype(jnp.bfloat16)
    place = lax.broadcasted_iota(jnp.int32, (docs, WIDE), 0).astype(jnp.float32) * MOST
    carry = jnp.zeros((docs, 1), jnp.float32)
    slot_parts = []
    for t in range(tokens // WIDE):
        match = own_t == ids[:, t * WIDE:(t + 1) * WIDE]
        hot = jnp.where(match, 1.0, 0.0)
        before = jnp.dot(hot.astype(jnp.bfloat16), before_t, preferred_element_type=jnp.float32)
        slot_parts.append(jnp.sum(jnp.where(match, place + before + carry, 0.0), axis=0, keepdims=True))
        carry = carry + jnp.sum(hot, axis=1, keepdims=True)
    slot = jnp.concatenate(slot_parts, axis=1).astype(jnp.int32)
    small[2].wait()
    small[3].wait()
    token_rows = jnp.concatenate([act_ref[...], grad_ref[...]], axis=0)

    def a2a(c, k, dest, src):
        return pltpu.make_async_remote_copy(
            src_ref=send.at[2 * c + k], dst_ref=recv.at[src], send_sem=sa,
            recv_sem=ra.at[c], device_id={"blk": dest}, device_id_type=pl.DeviceIdType.MESH)

    line = lax.broadcasted_iota(jnp.int32, (2 * slots, tokens), 0)
    for c in order + [0]:
        to = onto(c)
        hot = jnp.where(line == slot - to * (2 * slots), 1.0, 0.0).astype(jnp.bfloat16)
        packed = lax.dot_general(token_rows, hot, NT, preferred_element_type=jnp.float32).astype(jnp.bfloat16)
        halves = [packed[:, :slots], packed[:, slots:]]
        if c == order[0]:

            @pl.when(core == 0)
            def _():
                pl.semaphore_wait(barrier, blocks - 1)
                pl.semaphore_signal(go, inc=1, device_id={"blk": mate}, device_id_type=pl.DeviceIdType.MESH)

            @pl.when(core == 1)
            def _():
                pl.semaphore_wait(go, 1)

        if c:
            for k in range(2):
                send[2 * c + k] = halves[k]
                a2a(c, k, to * 2 + k, blk).start()
        else:
            first = core == 0
            send[0] = jnp.where(first, halves[1], halves[0])
            a2a(0, 0, mate, blk).start()
            recv[blk] = jnp.where(first, halves[0], halves[1])
    for load in loads:
        load.start()

    @pl.when(core == 1)
    def _():
        for d in range(1, mods):
            pl.semaphore_signal(barrier, inc=1, device_id={"mod": lax.rem(mod + d, mods)}, device_id_type=pl.DeviceIdType.MESH)


    row_w = lax.broadcasted_iota(jnp.int32, (WIDE, WIDE), 0)
    col_w = lax.broadcasted_iota(jnp.int32, (WIDE, WIDE), 1)
    small[4].wait()
    small[5].wait()
    tall = jnp.concatenate([pre_in_ref[...]] * band, axis=0)
    right = jnp.where(row_w // a_dim == col_w // a_dim, jnp.concatenate([tall] * band, axis=1), 0.0)
    high = right.astype(jnp.bfloat16)
    low = (right - high.astype(jnp.float32)).astype(jnp.bfloat16)
    kin[...] = jnp.concatenate([high, high, low], axis=0)
    left = jnp.concatenate([pre_out_ref[pl.ds(i, steps, stride=packs), :] for i in range(packs)], axis=0)
    wide_left = jnp.concatenate([left] * groups, axis=0)
    row_q = lax.broadcasted_iota(jnp.int32, (groups * g_dim, groups * g_dim), 0)
    col_q = lax.broadcasted_iota(jnp.int32, (groups * g_dim, groups * g_dim), 1)
    wide_left = jnp.where(row_q // g_dim == col_q // g_dim, jnp.concatenate([wide_left] * groups, axis=1), 0.0)
    high = wide_left.astype(jnp.bfloat16)
    low = (wide_left - high.astype(jnp.float32)).astype(jnp.bfloat16)
    kout[...] = jnp.concatenate([high, high, low], axis=1)
    spread = (
        lax.broadcasted_iota(jnp.int32, (a_dim, WIDE), 0) == lax.broadcasted_iota(jnp.int32, (a_dim, WIDE), 1) % a_dim
    ).astype(jnp.float32).astype(jnp.bfloat16)
    span = band * MOST
    slot_doc = (lax.broadcasted_iota(jnp.int32, (slots, WIDE), 0) % span) // MOST
    in_doc = (slot_doc == lax.broadcasted_iota(jnp.int32, (slots, WIDE), 1) // a_dim).astype(jnp.float32)
    slot_group = lax.broadcasted_iota(jnp.int32, (g_dim, slots), 1) // span
    in_group = [(slot_group == q).astype(jnp.float32).astype(jnp.bfloat16) for q in range(groups)]

    def wait_tokens(c):
        got = recv.at[pl.ds(source(c) * 2, 2)] if c else recv.at[mate]
        pltpu.make_async_copy(got, got, ra.at[c]).wait()

    doc_grad = None
    for c in [0] + order:
        wait_tokens(c)
        rights, lefts = [], []
        for k in range(2):
            s = source(c) * 2 + k
            wide = lax.dot_general(recv[s, :a_dim, :], spread, TN, preferred_element_type=jnp.float32)
            rights.append((wide * in_doc).astype(jnp.bfloat16))
            y = recv[s, a_dim:, :]
            lefts.append(jnp.concatenate([y * m for m in in_group], axis=0))
        part_grad = jnp.dot(
            jnp.concatenate(lefts, axis=1), jnp.concatenate(rights, axis=0), preferred_element_type=jnp.float32)
        doc_grad = part_grad if doc_grad is None else doc_grad + part_grad
    high = doc_grad.astype(jnp.bfloat16)
    low = (doc_grad - high.astype(jnp.float32)).astype(jnp.bfloat16)
    half = jnp.dot(jnp.concatenate([high, low, high], axis=1), kin[...], preferred_element_type=jnp.float32)
    high = half.astype(jnp.bfloat16)
    low = (half - high.astype(jnp.float32)).astype(jnp.bfloat16)
    cond = jnp.dot(kout[...], jnp.concatenate([high, low, high], axis=0), preferred_element_type=jnp.float32)

    rows = groups * steps
    lane_pack = lax.broadcasted_iota(jnp.int32, (rows, LANES), 1) // a_dim
    for side in range(WIDE // LANES):
        outs = [None] * packs
        for i in range(packs):
            x = jnp.concatenate(
                [cond[q * g_dim + i * steps:q * g_dim + (i + 1) * steps, side * LANES:(side + 1) * LANES]
                 for q in range(groups)], axis=0)
            for pos in range(packs):
                turn = ((i - pos) % packs) * a_dim
                moved = pltpu.roll(x, turn, 1) if turn else x
                outs[pos] = moved if outs[pos] is None else jnp.where(lane_pack == i, moved, outs[pos])
        for pos in range(packs):
            lay[pl.ds((side * packs + pos) * rows, rows), :] = outs[pos]

    def block_rows(b):
        return pl.ds(pl.multiple_of(b * per, per), per)

    def block(ch, b):
        return gath.at[ch, block_rows(b)]

    def move(ref, to, got):
        pltpu.make_async_remote_copy(
            src_ref=ref, dst_ref=ref, send_sem=sg, recv_sem=got, device_id={"blk": to},
            device_id_type=pl.DeviceIdType.MESH).start()

    def wait_for(ref, sem):
        pltpu.make_async_copy(ref, ref, sem).wait()

    squares = jnp.zeros((per, LANES), jnp.float32)
    per_chunk = part // LANES
    for ch in range(CHUNKS):
        for u in range(per_chunk):
            j = ch * per_chunk + u
            tile = jnp.concatenate(
                [lay[pl.ds(q * steps + j, band, stride=rows), :] for q in range(groups)], axis=0)
            squares = squares + tile * tile
            gath[ch, block_rows(blk), pl.ds(u * LANES, LANES)] = tile.astype(jnp.bfloat16)
        for c in order:
            move(block(ch, blk), onto(c) * 2 + core, rg.at[ch, c])
        move(block(ch, blk), mate, rp.at[ch])
    sq_out[...] = jnp.broadcast_to(jnp.sum(squares, axis=1, keepdims=True), (per, LANES))

    def square_copy(d):
        return pltpu.make_async_remote_copy(
            src_ref=sq_out, dst_ref=sq_in.at[d], send_sem=sn, recv_sem=rn,
            device_id={"mod": lax.rem(mod + d, mods)}, device_id_type=pl.DeviceIdType.MESH)

    def total_copy(d, src):
        return pltpu.make_async_remote_copy(
            src_ref=tot, dst_ref=norms.at[block_rows(src)], send_sem=st, recv_sem=rt,
            device_id={"blk": lax.rem(blk + d, blocks)}, device_id_type=pl.DeviceIdType.MESH)

    @pl.when(core == 1)
    def _():
        pl.semaphore_wait(barrier, mods - 1)
        pl.semaphore_signal(go, inc=1, device_id={"blk": mate}, device_id_type=pl.DeviceIdType.MESH)

    @pl.when(core == 0)
    def _():
        pl.semaphore_wait(go, 1)

    for d in range(1, mods):
        square_copy(d).start()

    def forward(ch, c):
        b = source(c) * 2 + core
        wait_for(block(ch, b), rg.at[ch, c])
        move(block(ch, b), mate, rp.at[ch])

    def multiply(ch):
        half_of = gath.at[ch, pl.ds(0, docs // 2)]
        wait_for(half_of, rp.at[ch])
        if ch == 0:
            pltpu.make_async_copy(train_ref, train_v, t_sem).wait()

        @pl.loop(0, tiles, unroll=UNROLL)
        def _(i):
            at = pl.ds(pl.multiple_of(i * WIDE, WIDE), WIDE)
            product = lax.dot_general(
                gath[ch], train_v[at, ch * part:(ch + 1) * part], NT, preferred_element_type=jnp.float32)
            if ch == 0:
                acc[:, at] = product
            elif ch < CHUNKS - 1:
                acc[:, at] = acc[:, at] + product
            else:
                acc[:, at] = (acc[:, at] + product) * inv[...]

    def totals():
        wait_for(sq_in.at[pl.ds(1, mods - 1)], rn)
        total = sq_out[...]
        for d in range(1, mods):
            total = total + sq_in[d]
        tot[...] = total
        norms[block_rows(blk), :] = total
        for d in range(1, blocks):
            total_copy(d, blk).start()

    for ch in range(CHUNKS):
        for at in range(ch + (ch > 0), min(ch + 2, CHUNKS)):
            for c in order:
                forward(at, c)
        if ch == 0:
            totals()
        if ch == CHUNKS - 1:
            others = norms.at[pl.ds(0, docs - per)]
            wait_for(others, rt)
            scale = 1.0 / jnp.sqrt(norms[...] + 1e-06)
            inv[...] = jnp.concatenate([scale] * (WIDE // LANES), axis=1)
        multiply(ch)
    wait_for(send.at[pl.ds(0, blocks - 1)], sa)
    wait_for(gath.at[:, pl.ds(0, docs - per)], sg)
    wait_for(sq_in.at[pl.ds(1, mods - 1)], sn)
    wait_for(others, st)


def body(blocks, mods, act, grad, train, pre_out, pre_in, doc_ids, owners):
    a_dim, tokens = act.shape[1:]
    g_dim = grad.shape[1]
    docs = owners.shape[0]
    per = docs // blocks
    chips = blocks // 2
    feats = a_dim * g_dim
    part = feats // CHUNKS
    rows = train.shape[1]
    tiles = rows // WIDE
    slots = per * MOST
    band = WIDE // a_dim
    square_of = per // band * g_dim
    hbm = pl.BlockSpec(memory_space=pltpu.HBM)
    dma = pltpu.SemaphoreType.DMA
    scores = pl.pallas_call(
        functools.partial(kernel, blocks, mods),
        out_shape=pltpu.VMEM((docs, rows), jnp.float32),
        in_specs=[hbm] * 7,
        out_specs=pl.BlockSpec(memory_space=pltpu.VMEM),
        scratch_shapes=[
            pltpu.VMEM((docs, LANES), jnp.float32),
            pltpu.VMEM((docs, WIDE), jnp.float32),
            pltpu.VMEM((square_of, 3 * square_of), jnp.bfloat16),
            pltpu.VMEM((1, tokens), jnp.int32),
            pltpu.VMEM((1, docs), jnp.int32),
            pltpu.VMEM((a_dim, tokens), jnp.bfloat16),
            pltpu.VMEM((g_dim, tokens), jnp.bfloat16),
            pltpu.VMEM((g_dim, g_dim), jnp.float32),
            pltpu.VMEM((a_dim, a_dim), jnp.float32),
            pltpu.VMEM((rows, feats), jnp.bfloat16),
            pltpu.VMEM((blocks, a_dim + g_dim, slots), jnp.bfloat16),
            pltpu.VMEM((blocks, a_dim + g_dim, slots), jnp.bfloat16),
            pltpu.VMEM((3 * WIDE, WIDE), jnp.bfloat16),
            pltpu.VMEM((per * g_dim * a_dim // LANES, LANES), jnp.float32),
            pltpu.VMEM((CHUNKS, docs, part), jnp.bfloat16),
            pltpu.VMEM((per, LANES), jnp.float32),
            pltpu.VMEM((mods, per, LANES), jnp.float32),
            pltpu.VMEM((per, LANES), jnp.float32),
            dma(()), dma((6,)), pltpu.SemaphoreType.REGULAR,
            dma(()), dma((chips,)),
            dma(()), dma((CHUNKS, chips)), dma((CHUNKS,)),
            dma(()), dma(()), dma(()), dma(()),
        ],
        compiler_params=pltpu.CompilerParams(
            collective_id=0, has_side_effects=True, vmem_limit_bytes=48 * 1024 * 1024),
    )(*[pltpu.with_memory_space_constraint(x, pltpu.HBM) for x in (
        doc_ids.reshape(1, tokens), owners.reshape(1, docs), act[0], grad[0], pre_out[0], pre_in[0], train[0])])
    return scores[None]


def solution(mesh):
    blocks, mods = mesh.shape["blk"], mesh.shape["mod"]
    return jax.shard_map(
        functools.partial(body, blocks, mods),
        mesh=mesh,
        in_specs=(
            P("mod", None, "blk"),
            P("mod", None, "blk"),
            P("mod", "blk", None),
            P("mod", None, None),
            P("mod", None, None),
            P("blk", None),
            P(),
        ),
        out_specs=P("mod", None, "blk"),
        check_vma=False,
    )
```

```python
import functools

import jax
import jax.numpy as jnp
from jax import lax
from jax.experimental import pallas as pl
from jax.experimental.pallas import tpu as pltpu
from jax.sharding import PartitionSpec as P

MOST = 4
LANES = 128
SUBLANES = 8
WIDE = 256
CHUNKS = 4
UNROLL = 8
NT = (((1,), (1,)), ((), ()))
TN = (((0,), (0,)), ((), ()))
HIGH = lax.Precision.HIGHEST


def kernel(
    blocks, mods,
    ids_hbm, own_hbm, act_hbm, grad_hbm, pre_out_hbm, pre_in_hbm, train_ref,
    acc, norms, inv, kout, ids_ref, own_ref, act_ref, grad_ref, pre_out_ref, pre_in_ref, train_v, send, recv, kin, lay, gath, sq_out, sq_in, tot,
    t_sem, i_sem, go, sa, ra, sg, rg, rp, sn, rn, st, rt,
):
    a_dim, tokens = act_hbm.shape
    g_dim = grad_hbm.shape[0]
    docs = own_hbm.shape[1]
    per = docs // blocks
    slots = per * MOST
    chips = blocks // 2
    feats = a_dim * g_dim
    part = feats // CHUNKS
    rows_all = train_ref.shape[0]
    tiles = rows_all // WIDE
    packs = LANES // a_dim
    band = WIDE // a_dim
    groups = per // band
    steps = g_dim // packs

    blk = lax.axis_index("blk")
    mod = lax.axis_index("mod")
    chip = lax.div(blk, 2)
    core = lax.rem(blk, 2)
    mate = chip * 2 + (1 - core)
    square = chips == 4
    if square:
        hops = [chip, chip + 1 - 2 * lax.rem(chip, 2), lax.rem(chip + 2, chips), chips - 1 - chip]

    def onto(c):
        return hops[c] if square else lax.rem(chip + c, chips)

    def source(c):
        return hops[c] if square else lax.rem(chip - c + chips, chips)

    order = list(range(chips - 1, 0, -1))

    loads = [
        pltpu.make_async_copy(
            train_ref.at[pl.ds(i * WIDE, WIDE)], train_v.at[pl.ds(i * WIDE, WIDE)], t_sem
        )
        for i in range(tiles)
    ]
    small = [
        pltpu.make_async_copy(src, dst, i_sem.at[i])
        for i, (src, dst) in enumerate((
            (ids_hbm, ids_ref), (own_hbm, own_ref), (act_hbm, act_ref),
            (grad_hbm, grad_ref), (pre_out_hbm, pre_out_ref), (pre_in_hbm, pre_in_ref)))
    ]
    for load in small:
        load.start()
    barrier = pltpu.get_barrier_semaphore()
    for c in range(chips):
        @pl.when(c * 2 != blk)
        def _():
            pl.semaphore_signal(barrier, inc=1, device_id={"blk": c * 2}, device_id_type=pl.DeviceIdType.MESH)
    small[0].wait()
    small[1].wait()

    ids = ids_ref[...].astype(jnp.float32)
    own_t = jnp.transpose(jnp.broadcast_to(own_ref[...].astype(jnp.float32), (WIDE, docs)))
    before_t = (
        lax.broadcasted_iota(jnp.int32, (WIDE, WIDE), 0) < lax.broadcasted_iota(jnp.int32, (WIDE, WIDE), 1)
    ).astype(jnp.float32).astype(jnp.bfloat16)
    place = lax.broadcasted_iota(jnp.int32, (docs, WIDE), 0).astype(jnp.float32) * MOST
    carry = jnp.zeros((docs, 1), jnp.float32)
    slot_parts = []
    for t in range(tokens // WIDE):
        match = own_t == ids[:, t * WIDE:(t + 1) * WIDE]
        hot = jnp.where(match, 1.0, 0.0)
        before = jnp.dot(hot.astype(jnp.bfloat16), before_t, preferred_element_type=jnp.float32)
        slot_parts.append(jnp.sum(jnp.where(match, place + before + carry, 0.0), axis=0, keepdims=True))
        carry = carry + jnp.sum(hot, axis=1, keepdims=True)
    slot = jnp.concatenate(slot_parts, axis=1).astype(jnp.int32)
    small[2].wait()
    small[3].wait()
    token_rows = jnp.concatenate([act_ref[...], grad_ref[...]], axis=0)

    def a2a(c, k, dest, src):
        return pltpu.make_async_remote_copy(
            src_ref=send.at[2 * c + k], dst_ref=recv.at[src], send_sem=sa,
            recv_sem=ra.at[c], device_id={"blk": dest}, device_id_type=pl.DeviceIdType.MESH)

    line = lax.broadcasted_iota(jnp.int32, (2 * slots, tokens), 0).astype(jnp.float32).astype(jnp.bfloat16)
    one, zero = jnp.ones((), jnp.bfloat16), jnp.zeros((), jnp.bfloat16)
    for c in order + [0]:
        to = onto(c)
        mine = jnp.clip(slot - to * (2 * slots), -1, 2 * slots).astype(jnp.float32).astype(jnp.bfloat16)
        hot = jnp.where(line == mine, one, zero)
        packed = lax.dot_general(token_rows, hot, NT, preferred_element_type=jnp.float32).astype(jnp.bfloat16)
        halves = [packed[:, :slots], packed[:, slots:]]
        if c == order[0]:

            @pl.when(core == 0)
            def _():
                pl.semaphore_wait(barrier, blocks - 1)
                pl.semaphore_signal(go, inc=1, device_id={"blk": mate}, device_id_type=pl.DeviceIdType.MESH)

            @pl.when(core == 1)
            def _():
                pl.semaphore_wait(go, 1)

        if c:
            for k in range(2):
                send[2 * c + k] = halves[k]
                a2a(c, k, to * 2 + k, blk).start()
        else:
            first = core == 0
            send[0] = jnp.where(first, halves[1], halves[0])
            a2a(0, 0, mate, blk).start()
            recv[blk] = jnp.where(first, halves[0], halves[1])
    for load in loads:
        load.start()

    @pl.when(core == 1)
    def _():
        for d in range(1, mods):
            pl.semaphore_signal(barrier, inc=1, device_id={"mod": lax.rem(mod + d, mods)}, device_id_type=pl.DeviceIdType.MESH)


    row_w = lax.broadcasted_iota(jnp.int32, (WIDE, WIDE), 0)
    col_w = lax.broadcasted_iota(jnp.int32, (WIDE, WIDE), 1)
    small[4].wait()
    small[5].wait()
    tall = jnp.concatenate([pre_in_ref[...]] * band, axis=0)
    right = jnp.where(row_w // a_dim == col_w // a_dim, jnp.concatenate([tall] * band, axis=1), 0.0)
    high = right.astype(jnp.bfloat16)
    low = (right - high.astype(jnp.float32)).astype(jnp.bfloat16)
    kin[...] = jnp.concatenate([high, high, low], axis=0)
    left = jnp.concatenate([pre_out_ref[pl.ds(i, steps, stride=packs), :] for i in range(packs)], axis=0)
    wide_left = jnp.concatenate([left] * groups, axis=0)
    row_q = lax.broadcasted_iota(jnp.int32, (groups * g_dim, groups * g_dim), 0)
    col_q = lax.broadcasted_iota(jnp.int32, (groups * g_dim, groups * g_dim), 1)
    wide_left = jnp.where(row_q // g_dim == col_q // g_dim, jnp.concatenate([wide_left] * groups, axis=1), 0.0)
    high = wide_left.astype(jnp.bfloat16)
    low = (wide_left - high.astype(jnp.float32)).astype(jnp.bfloat16)
    kout[...] = jnp.concatenate([high, high, low], axis=1)
    spread = (
        lax.broadcasted_iota(jnp.int32, (a_dim, WIDE), 0) == lax.broadcasted_iota(jnp.int32, (a_dim, WIDE), 1) % a_dim
    ).astype(jnp.float32).astype(jnp.bfloat16)
    span = band * MOST
    slot_doc = (lax.broadcasted_iota(jnp.int32, (slots, WIDE), 0) % span) // MOST
    in_doc = (slot_doc == lax.broadcasted_iota(jnp.int32, (slots, WIDE), 1) // a_dim).astype(jnp.float32)
    slot_group = lax.broadcasted_iota(jnp.int32, (g_dim, slots), 1) // span
    in_group = [(slot_group == q).astype(jnp.float32).astype(jnp.bfloat16) for q in range(groups)]

    def wait_tokens(c):
        got = recv.at[pl.ds(source(c) * 2, 2)] if c else recv.at[mate]
        pltpu.make_async_copy(got, got, ra.at[c]).wait()

    doc_grad = None
    for c in [0] + order:
        wait_tokens(c)
        rights, lefts = [], []
        for k in range(2):
            s = source(c) * 2 + k
            wide = lax.dot_general(recv[s, :a_dim, :], spread, TN, preferred_element_type=jnp.float32)
            rights.append((wide * in_doc).astype(jnp.bfloat16))
            y = recv[s, a_dim:, :]
            lefts.append(jnp.concatenate([y * m for m in in_group], axis=0))
        part_grad = jnp.dot(
            jnp.concatenate(lefts, axis=1), jnp.concatenate(rights, axis=0), preferred_element_type=jnp.float32)
        doc_grad = part_grad if doc_grad is None else doc_grad + part_grad
    high = doc_grad.astype(jnp.bfloat16)
    low = (doc_grad - high.astype(jnp.float32)).astype(jnp.bfloat16)
    half = jnp.dot(jnp.concatenate([high, low, high], axis=1), kin[...], preferred_element_type=jnp.float32)
    high = half.astype(jnp.bfloat16)
    low = (half - high.astype(jnp.float32)).astype(jnp.bfloat16)
    cond = jnp.dot(kout[...], jnp.concatenate([high, low, high], axis=0), preferred_element_type=jnp.float32)

    rows = groups * steps
    lane_pack = lax.broadcasted_iota(jnp.int32, (rows, LANES), 1) // a_dim
    for side in range(WIDE // LANES):
        outs = [None] * packs
        for i in range(packs):
            x = jnp.concatenate(
                [cond[q * g_dim + i * steps:q * g_dim + (i + 1) * steps, side * LANES:(side + 1) * LANES]
                 for q in range(groups)], axis=0)
            for pos in range(packs):
                turn = ((i - pos) % packs) * a_dim
                moved = pltpu.roll(x, turn, 1) if turn else x
                outs[pos] = moved if outs[pos] is None else jnp.where(lane_pack == i, moved, outs[pos])
        for pos in range(packs):
            lay[pl.ds((side * packs + pos) * rows, rows), :] = outs[pos]

    def block_rows(b):
        return pl.ds(pl.multiple_of(b * per, per), per)

    def block(ch, b):
        return gath.at[ch, block_rows(b)]

    def move(ref, to, got):
        pltpu.make_async_remote_copy(
            src_ref=ref, dst_ref=ref, send_sem=sg, recv_sem=got, device_id={"blk": to},
            device_id_type=pl.DeviceIdType.MESH).start()

    def wait_for(ref, sem):
        pltpu.make_async_copy(ref, ref, sem).wait()

    squares = jnp.zeros((per, LANES), jnp.float32)
    per_chunk = part // LANES
    for ch in range(CHUNKS):
        for u in range(per_chunk):
            j = ch * per_chunk + u
            tile = jnp.concatenate(
                [lay[pl.ds(q * steps + j, band, stride=rows), :] for q in range(groups)], axis=0)
            squares = squares + tile * tile
            gath[ch, block_rows(blk), pl.ds(u * LANES, LANES)] = tile.astype(jnp.bfloat16)
        for c in order:
            move(block(ch, blk), onto(c) * 2 + core, rg.at[ch, c - 1])
        move(block(ch, blk), mate, rp.at[ch])
    diagonal = lax.broadcasted_iota(jnp.int32, (per, LANES), 0) == lax.broadcasted_iota(jnp.int32, (per, LANES), 1)
    squares = jnp.broadcast_to(jnp.sum(squares, axis=1, keepdims=True), (per, LANES))
    sq_out[...] = jnp.broadcast_to(
        jnp.sum(jnp.where(diagonal, squares, 0.0), axis=0, keepdims=True), (SUBLANES, LANES))

    def square_copy(d):
        return pltpu.make_async_remote_copy(
            src_ref=sq_out, dst_ref=sq_in.at[d], send_sem=sn, recv_sem=rn,
            device_id={"mod": lax.rem(mod + d, mods)}, device_id_type=pl.DeviceIdType.MESH)

    def total_copy(d, src):
        return pltpu.make_async_remote_copy(
            src_ref=tot, dst_ref=norms.at[src], send_sem=st, recv_sem=rt,
            device_id={"blk": lax.rem(blk + d, blocks)}, device_id_type=pl.DeviceIdType.MESH)

    @pl.when(core == 1)
    def _():
        pl.semaphore_wait(barrier, mods - 1)
        pl.semaphore_signal(go, inc=1, device_id={"blk": mate}, device_id_type=pl.DeviceIdType.MESH)

    @pl.when(core == 0)
    def _():
        pl.semaphore_wait(go, 1)

    for d in range(1, mods):
        square_copy(d).start()

    def forward(ch, c):
        b = source(c) * 2 + core
        wait_for(block(ch, b), rg.at[ch, c - 1])
        move(block(ch, b), mate, rp.at[ch])

    def multiply(ch):
        half_of = gath.at[ch, pl.ds(0, docs // 2)]
        wait_for(half_of, rp.at[ch])
        if ch == 0:
            pltpu.make_async_copy(train_ref, train_v, t_sem).wait()

        @pl.loop(0, tiles, unroll=UNROLL)
        def _(i):
            at = pl.ds(pl.multiple_of(i * WIDE, WIDE), WIDE)
            product = lax.dot_general(
                gath[ch], train_v[at, ch * part:(ch + 1) * part], NT, preferred_element_type=jnp.float32)
            if ch == 0:
                acc[:, at] = product
            elif ch < CHUNKS - 1:
                acc[:, at] = acc[:, at] + product
            else:
                acc[:, at] = (acc[:, at] + product) * inv[...]

    def totals():
        wait_for(sq_in.at[pl.ds(1, mods - 1)], rn)
        total = sq_out[...]
        for d in range(1, mods):
            total = total + sq_in[d]
        tot[...] = total
        norms[blk] = total
        for d in range(1, blocks):
            total_copy(d, blk).start()

    for ch in range(CHUNKS):
        for at in range(ch + (ch > 0), min(ch + 2, CHUNKS)):
            for c in order[1:] + order[:1]:
                forward(at, c)
        if ch == 0:
            totals()
        if ch == CHUNKS - 1:
            others = norms.at[pl.ds(0, blocks - 1)]
            wait_for(others, rt)
            for b in range(blocks):
                row = jnp.broadcast_to(norms[b, :1, :], (per, LANES))
                total = jnp.sum(jnp.where(diagonal, row, 0.0), axis=1, keepdims=True)
                inv[b * per:(b + 1) * per, :] = jnp.broadcast_to(1.0 / jnp.sqrt(total + 1e-06), (per, WIDE))
        multiply(ch)
    wait_for(send.at[pl.ds(0, blocks - 1)], sa)
    wait_for(gath.at[:, pl.ds(0, docs - per)], sg)
    wait_for(sq_in.at[pl.ds(1, mods - 1)], sn)
    wait_for(others, st)


def body(blocks, mods, act, grad, train, pre_out, pre_in, doc_ids, owners):
    a_dim, tokens = act.shape[1:]
    g_dim = grad.shape[1]
    docs = owners.shape[0]
    per = docs // blocks
    chips = blocks // 2
    feats = a_dim * g_dim
    part = feats // CHUNKS
    rows = train.shape[1]
    tiles = rows // WIDE
    slots = per * MOST
    band = WIDE // a_dim
    square_of = per // band * g_dim
    hbm = pl.BlockSpec(memory_space=pltpu.HBM)
    dma = pltpu.SemaphoreType.DMA
    scores = pl.pallas_call(
        functools.partial(kernel, blocks, mods),
        out_shape=pltpu.VMEM((docs, rows), jnp.float32),
        in_specs=[hbm] * 7,
        out_specs=pl.BlockSpec(memory_space=pltpu.VMEM),
        scratch_shapes=[
            pltpu.VMEM((blocks, SUBLANES, LANES), jnp.float32),
            pltpu.VMEM((docs, WIDE), jnp.float32),
            pltpu.VMEM((square_of, 3 * square_of), jnp.bfloat16),
            pltpu.VMEM((1, tokens), jnp.int32),
            pltpu.VMEM((1, docs), jnp.int32),
            pltpu.VMEM((a_dim, tokens), jnp.bfloat16),
            pltpu.VMEM((g_dim, tokens), jnp.bfloat16),
            pltpu.VMEM((g_dim, g_dim), jnp.float32),
            pltpu.VMEM((a_dim, a_dim), jnp.float32),
            pltpu.VMEM((rows, feats), jnp.bfloat16),
            pltpu.VMEM((blocks, a_dim + g_dim, slots), jnp.bfloat16),
            pltpu.VMEM((blocks, a_dim + g_dim, slots), jnp.bfloat16),
            pltpu.VMEM((3 * WIDE, WIDE), jnp.bfloat16),
            pltpu.VMEM((per * g_dim * a_dim // LANES, LANES), jnp.float32),
            pltpu.VMEM((CHUNKS, docs, part), jnp.bfloat16),
            pltpu.VMEM((SUBLANES, LANES), jnp.float32),
            pltpu.VMEM((mods, SUBLANES, LANES), jnp.float32),
            pltpu.VMEM((SUBLANES, LANES), jnp.float32),
            dma(()), dma((6,)), pltpu.SemaphoreType.REGULAR,
            dma(()), dma((chips,)),
            dma(()), dma((CHUNKS, chips - 1)), dma((CHUNKS,)),
            dma(()), dma(()), dma(()), dma(()),
        ],
        compiler_params=pltpu.CompilerParams(
            collective_id=0, has_side_effects=True, vmem_limit_bytes=48 * 1024 * 1024),
    )(*[pltpu.with_memory_space_constraint(x, pltpu.HBM) for x in (
        doc_ids.reshape(1, tokens), owners.reshape(1, docs), act[0], grad[0], pre_out[0], pre_in[0], train[0])])
    return scores[None]


def solution(mesh):
    blocks, mods = mesh.shape["blk"], mesh.shape["mod"]
    return jax.shard_map(
        functools.partial(body, blocks, mods),
        mesh=mesh,
        in_specs=(
            P("mod", None, "blk"),
            P("mod", None, "blk"),
            P("mod", "blk", None),
            P("mod", None, None),
            P("mod", None, None),
            P("blk", None),
            P(),
        ),
        out_specs=P("mod", None, "blk"),
        check_vma=False,
    )
```

```python
import functools

import jax
import jax.numpy as jnp
from jax import lax
from jax.experimental import pallas as pl
from jax.experimental.pallas import tpu as pltpu
from jax.sharding import PartitionSpec as P

MOST = 4
LANES = 128
HALVES = 2
SUBLANES = 8
WIDE = 256
CHUNKS = 4
UNROLL = 8
NT = (((1,), (1,)), ((), ()))
TN = (((0,), (0,)), ((), ()))


def kernel(
    blocks, mods,
    ids_hbm, own_hbm, act_hbm, grad_hbm, pre_out_hbm, pre_in_hbm, train_ref,
    acc, norms, inv, kout, ids_ref, own_ref, act_ref, grad_ref, pre_out_ref, pre_in_ref, train_v, send, recv, kin, lay, gath, sq_out, sq_in, tot,
    t_sem, i_sem, go, sa, ra, sg, rg, rp, sn, rn, st, rt,
):
    a_dim, tokens = act_hbm.shape
    g_dim = grad_hbm.shape[0]
    docs = own_hbm.shape[1]
    per = docs // blocks
    slots = per * MOST
    chips = blocks // 2
    feats = a_dim * g_dim
    part = feats // CHUNKS
    rows_all = train_ref.shape[0]
    tiles = rows_all // WIDE
    packs = LANES // a_dim
    band = WIDE // a_dim
    groups = per // band
    steps = g_dim // packs

    blk = lax.axis_index("blk")
    mod = lax.axis_index("mod")
    chip = lax.div(blk, 2)
    core = lax.rem(blk, 2)
    mate = chip * 2 + (1 - core)
    square = chips == 4
    if square:
        hops = [chip, chip + 1 - 2 * lax.rem(chip, 2), lax.rem(chip + 2, chips), chips - 1 - chip]

    def onto(c):
        return hops[c] if square else lax.rem(chip + c, chips)

    def source(c):
        return hops[c] if square else lax.rem(chip - c + chips, chips)

    order = list(range(chips - 1, 0, -1))

    loads = [
        pltpu.make_async_copy(
            train_ref.at[pl.ds(i * WIDE, WIDE)], train_v.at[pl.ds(i * WIDE, WIDE)], t_sem
        )
        for i in range(tiles)
    ]
    small = [
        pltpu.make_async_copy(src, dst, i_sem.at[i])
        for i, (src, dst) in enumerate((
            (ids_hbm, ids_ref), (own_hbm, own_ref), (act_hbm, act_ref),
            (grad_hbm, grad_ref), (pre_out_hbm, pre_out_ref), (pre_in_hbm, pre_in_ref)))
    ]
    for load in small:
        load.start()
    barrier = pltpu.get_barrier_semaphore()
    for c in range(chips):
        @pl.when(c * 2 != blk)
        def _():
            pl.semaphore_signal(barrier, inc=1, device_id={"blk": c * 2}, device_id_type=pl.DeviceIdType.MESH)
    small[0].wait()
    small[1].wait()

    ids = ids_ref[...].astype(jnp.float32)
    own_t = jnp.transpose(jnp.broadcast_to(own_ref[...].astype(jnp.float32), (WIDE, docs)))
    before_t = (
        lax.broadcasted_iota(jnp.int32, (WIDE, WIDE), 0) < lax.broadcasted_iota(jnp.int32, (WIDE, WIDE), 1)
    ).astype(jnp.float32).astype(jnp.bfloat16)
    place = lax.broadcasted_iota(jnp.int32, (docs, WIDE), 0).astype(jnp.float32) * MOST
    carry = jnp.zeros((docs, 1), jnp.float32)
    slot_parts = []
    for t in range(tokens // WIDE):
        match = own_t == ids[:, t * WIDE:(t + 1) * WIDE]
        hot = jnp.where(match, 1.0, 0.0)
        before = jnp.dot(hot.astype(jnp.bfloat16), before_t, preferred_element_type=jnp.float32)
        slot_parts.append(jnp.sum(jnp.where(match, place + before + carry, 0.0), axis=0, keepdims=True))
        carry = carry + jnp.sum(hot, axis=1, keepdims=True)
    slot = jnp.concatenate(slot_parts, axis=1).astype(jnp.int32)
    small[2].wait()
    small[3].wait()
    token_rows = jnp.concatenate([act_ref[...], grad_ref[...]], axis=0)

    def a2a(c, k, dest, src):
        return pltpu.make_async_remote_copy(
            src_ref=send.at[2 * c + k], dst_ref=recv.at[src], send_sem=sa,
            recv_sem=ra.at[c], device_id={"blk": dest}, device_id_type=pl.DeviceIdType.MESH)

    line = lax.broadcasted_iota(jnp.int32, (2 * slots, tokens), 0).astype(jnp.float32).astype(jnp.bfloat16)
    one, zero = jnp.ones((), jnp.bfloat16), jnp.zeros((), jnp.bfloat16)
    for c in order + [0]:
        to = onto(c)
        mine = jnp.clip(slot - to * (2 * slots), -1, 2 * slots).astype(jnp.float32).astype(jnp.bfloat16)
        hot = jnp.where(line == mine, one, zero)
        packed = lax.dot_general(token_rows, hot, NT, preferred_element_type=jnp.float32).astype(jnp.bfloat16)
        halves = [packed[:, :slots], packed[:, slots:]]
        if c == order[0]:

            @pl.when(core == 0)
            def _():
                pl.semaphore_wait(barrier, blocks - 1)
                pl.semaphore_signal(go, inc=1, device_id={"blk": mate}, device_id_type=pl.DeviceIdType.MESH)

            @pl.when(core == 1)
            def _():
                pl.semaphore_wait(go, 1)

        if c:
            for k in range(2):
                send[2 * c + k] = halves[k]
                a2a(c, k, to * 2 + k, blk).start()
        else:
            first = core == 0
            send[0] = jnp.where(first, halves[1], halves[0])
            a2a(0, 0, mate, blk).start()
            recv[blk] = jnp.where(first, halves[0], halves[1])
    for load in loads:
        load.start()

    @pl.when(core == 1)
    def _():
        for d in range(1, mods):
            pl.semaphore_signal(barrier, inc=1, device_id={"mod": lax.rem(mod + d, mods)}, device_id_type=pl.DeviceIdType.MESH)


    row_w = lax.broadcasted_iota(jnp.int32, (WIDE, WIDE), 0)
    col_w = lax.broadcasted_iota(jnp.int32, (WIDE, WIDE), 1)
    small[4].wait()
    small[5].wait()
    tall = jnp.concatenate([pre_in_ref[...]] * band, axis=0)
    right = jnp.where(row_w // a_dim == col_w // a_dim, jnp.concatenate([tall] * band, axis=1), 0.0)
    high = right.astype(jnp.bfloat16)
    low = (right - high.astype(jnp.float32)).astype(jnp.bfloat16)
    kin[...] = jnp.concatenate([high, high, low], axis=0)
    left = jnp.concatenate([pre_out_ref[pl.ds(i, steps, stride=packs), :] for i in range(packs)], axis=0)
    short = steps // HALVES
    bands = packs * short
    wide_left = jnp.concatenate(
        [left[i * steps + n * short:i * steps + (n + 1) * short]
         for n in range(HALVES) for _ in range(groups) for i in range(packs)], axis=0)
    row_q = lax.broadcasted_iota(jnp.int32, (groups * g_dim, groups * g_dim), 0)
    col_q = lax.broadcasted_iota(jnp.int32, (groups * g_dim, groups * g_dim), 1)
    wide_left = jnp.where(
        (row_q % (groups * bands)) // bands == col_q // g_dim, jnp.concatenate([wide_left] * groups, axis=1), 0.0)
    high = wide_left.astype(jnp.bfloat16)
    low = (wide_left - high.astype(jnp.float32)).astype(jnp.bfloat16)
    kout[...] = jnp.concatenate([high, high, low], axis=1)
    spread = (
        lax.broadcasted_iota(jnp.int32, (a_dim, WIDE), 0) == lax.broadcasted_iota(jnp.int32, (a_dim, WIDE), 1) % a_dim
    ).astype(jnp.float32).astype(jnp.bfloat16)
    span = band * MOST
    slot_doc = (lax.broadcasted_iota(jnp.int32, (slots, WIDE), 0) % span) // MOST
    in_doc = (slot_doc == lax.broadcasted_iota(jnp.int32, (slots, WIDE), 1) // a_dim).astype(jnp.float32)
    slot_group = lax.broadcasted_iota(jnp.int32, (g_dim, slots), 1) // span
    in_group = [(slot_group == q).astype(jnp.float32).astype(jnp.bfloat16) for q in range(groups)]

    def wait_tokens(c):
        got = recv.at[pl.ds(source(c) * 2, 2)] if c else recv.at[mate]
        pltpu.make_async_copy(got, got, ra.at[c]).wait()

    doc_grad = None
    for c in [0] + order:
        wait_tokens(c)
        rights, lefts = [], []
        for k in range(2):
            s = source(c) * 2 + k
            wide = lax.dot_general(recv[s, :a_dim, :], spread, TN, preferred_element_type=jnp.float32)
            rights.append((wide * in_doc).astype(jnp.bfloat16))
            y = recv[s, a_dim:, :]
            lefts.append(jnp.concatenate([y * m for m in in_group], axis=0))
        part_grad = jnp.dot(
            jnp.concatenate(lefts, axis=1), jnp.concatenate(rights, axis=0), preferred_element_type=jnp.float32)
        doc_grad = part_grad if doc_grad is None else doc_grad + part_grad
    high = doc_grad.astype(jnp.bfloat16)
    low = (doc_grad - high.astype(jnp.float32)).astype(jnp.bfloat16)
    half = jnp.dot(jnp.concatenate([high, low, high], axis=1), kin[...], preferred_element_type=jnp.float32)
    high = half.astype(jnp.bfloat16)
    low = (half - high.astype(jnp.float32)).astype(jnp.bfloat16)
    half = jnp.concatenate([high, low, high], axis=0)

    rows = groups * steps
    lane_pack = lax.broadcasted_iota(jnp.int32, (groups * short, LANES), 1) // a_dim

    def lay_out(n):
        cond = jnp.dot(kout[n * groups * bands:(n + 1) * groups * bands, :], half, preferred_element_type=jnp.float32)
        for side in range(WIDE // LANES):
            outs = [None] * packs
            for i in range(packs):
                x = jnp.concatenate(
                    [cond[q * bands + i * short:q * bands + (i + 1) * short, side * LANES:(side + 1) * LANES]
                     for q in range(groups)], axis=0)
                for pos in range(packs):
                    turn = ((i - pos) % packs) * a_dim
                    moved = pltpu.roll(x, turn, 1) if turn else x
                    outs[pos] = moved if outs[pos] is None else jnp.where(lane_pack == i, moved, outs[pos])
            for pos in range(packs):
                for q in range(groups):
                    lay[pl.ds((side * packs + pos) * rows + q * steps + n * short, short), :] = (
                        outs[pos][q * short:(q + 1) * short])

    def block_rows(b):
        return pl.ds(pl.multiple_of(b * per, per), per)

    def block(ch, b):
        return gath.at[ch, block_rows(b)]

    def move(ref, to, got):
        pltpu.make_async_remote_copy(
            src_ref=ref, dst_ref=ref, send_sem=sg, recv_sem=got, device_id={"blk": to},
            device_id_type=pl.DeviceIdType.MESH).start()

    def wait_for(ref, sem):
        pltpu.make_async_copy(ref, ref, sem).wait()

    squares = jnp.zeros((per, LANES), jnp.float32)
    per_chunk = part // LANES
    for ch in range(CHUNKS):
        if ch % (CHUNKS // HALVES) == 0:
            lay_out(ch // (CHUNKS // HALVES))
        for u in range(per_chunk):
            j = ch * per_chunk + u
            tile = jnp.concatenate(
                [lay[pl.ds(q * steps + j, band, stride=rows), :] for q in range(groups)], axis=0)
            squares = squares + tile * tile
            gath[ch, block_rows(blk), pl.ds(u * LANES, LANES)] = tile.astype(jnp.bfloat16)
        for c in order:
            move(block(ch, blk), onto(c) * 2 + core, rg.at[ch, c - 1])
        move(block(ch, blk), mate, rp.at[ch])
    diagonal = lax.broadcasted_iota(jnp.int32, (per, LANES), 0) == lax.broadcasted_iota(jnp.int32, (per, LANES), 1)
    squares = jnp.broadcast_to(jnp.sum(squares, axis=1, keepdims=True), (per, LANES))
    sq_out[...] = jnp.broadcast_to(
        jnp.sum(jnp.where(diagonal, squares, 0.0), axis=0, keepdims=True), (SUBLANES, LANES))

    def square_copy(d):
        return pltpu.make_async_remote_copy(
            src_ref=sq_out, dst_ref=sq_in.at[d], send_sem=sn, recv_sem=rn,
            device_id={"mod": lax.rem(mod + d, mods)}, device_id_type=pl.DeviceIdType.MESH)

    def total_copy(d, src):
        return pltpu.make_async_remote_copy(
            src_ref=tot, dst_ref=norms.at[src], send_sem=st, recv_sem=rt,
            device_id={"blk": lax.rem(blk + d, blocks)}, device_id_type=pl.DeviceIdType.MESH)

    @pl.when(core == 1)
    def _():
        pl.semaphore_wait(barrier, mods - 1)
        pl.semaphore_signal(go, inc=1, device_id={"blk": mate}, device_id_type=pl.DeviceIdType.MESH)

    @pl.when(core == 0)
    def _():
        pl.semaphore_wait(go, 1)

    for d in range(1, mods):
        square_copy(d).start()

    def forward(ch, c):
        b = source(c) * 2 + core
        wait_for(block(ch, b), rg.at[ch, c - 1])
        move(block(ch, b), mate, rp.at[ch])

    def multiply(ch):
        half_of = gath.at[ch, pl.ds(0, docs // 2)]
        wait_for(half_of, rp.at[ch])
        if ch == 0:
            pltpu.make_async_copy(train_ref, train_v, t_sem).wait()

        @pl.loop(0, tiles, unroll=UNROLL)
        def _(i):
            at = pl.ds(pl.multiple_of(i * WIDE, WIDE), WIDE)
            product = lax.dot_general(
                gath[ch], train_v[at, ch * part:(ch + 1) * part], NT, preferred_element_type=jnp.float32)
            if ch == 0:
                acc[:, at] = product
            elif ch < CHUNKS - 1:
                acc[:, at] = acc[:, at] + product
            else:
                acc[:, at] = (acc[:, at] + product) * inv[...]

    def totals():
        wait_for(sq_in.at[pl.ds(1, mods - 1)], rn)
        total = sq_out[...]
        for d in range(1, mods):
            total = total + sq_in[d]
        tot[...] = total
        norms[blk] = total
        for d in range(1, blocks):
            total_copy(d, blk).start()

    for ch in range(CHUNKS):
        for at in range(ch + (ch > 0), min(ch + 2, CHUNKS)):
            for c in order[1:] + order[:1]:
                forward(at, c)
        if ch == 0:
            totals()
        if ch == CHUNKS - 1:
            others = norms.at[pl.ds(0, blocks - 1)]
            wait_for(others, rt)
            for b in range(blocks):
                row = jnp.broadcast_to(norms[b, :1, :], (per, LANES))
                total = jnp.sum(jnp.where(diagonal, row, 0.0), axis=1, keepdims=True)
                inv[b * per:(b + 1) * per, :] = jnp.broadcast_to(1.0 / jnp.sqrt(total + 1e-06), (per, WIDE))
        multiply(ch)
    wait_for(send.at[pl.ds(0, blocks - 1)], sa)
    wait_for(gath.at[:, pl.ds(0, docs - per)], sg)
    wait_for(sq_in.at[pl.ds(1, mods - 1)], sn)
    wait_for(others, st)


def body(blocks, mods, act, grad, train, pre_out, pre_in, doc_ids, owners):
    a_dim, tokens = act.shape[1:]
    g_dim = grad.shape[1]
    docs = owners.shape[0]
    per = docs // blocks
    chips = blocks // 2
    feats = a_dim * g_dim
    part = feats // CHUNKS
    rows = train.shape[1]
    tiles = rows // WIDE
    slots = per * MOST
    band = WIDE // a_dim
    square_of = per // band * g_dim
    hbm = pl.BlockSpec(memory_space=pltpu.HBM)
    dma = pltpu.SemaphoreType.DMA
    scores = pl.pallas_call(
        functools.partial(kernel, blocks, mods),
        out_shape=pltpu.VMEM((docs, rows), jnp.float32),
        in_specs=[hbm] * 7,
        out_specs=pl.BlockSpec(memory_space=pltpu.VMEM),
        scratch_shapes=[
            pltpu.VMEM((blocks, SUBLANES, LANES), jnp.float32),
            pltpu.VMEM((docs, WIDE), jnp.float32),
            pltpu.VMEM((square_of, 3 * square_of), jnp.bfloat16),
            pltpu.VMEM((1, tokens), jnp.int32),
            pltpu.VMEM((1, docs), jnp.int32),
            pltpu.VMEM((a_dim, tokens), jnp.bfloat16),
            pltpu.VMEM((g_dim, tokens), jnp.bfloat16),
            pltpu.VMEM((g_dim, g_dim), jnp.float32),
            pltpu.VMEM((a_dim, a_dim), jnp.float32),
            pltpu.VMEM((rows, feats), jnp.bfloat16),
            pltpu.VMEM((blocks, a_dim + g_dim, slots), jnp.bfloat16),
            pltpu.VMEM((blocks, a_dim + g_dim, slots), jnp.bfloat16),
            pltpu.VMEM((3 * WIDE, WIDE), jnp.bfloat16),
            pltpu.VMEM((per * g_dim * a_dim // LANES, LANES), jnp.float32),
            pltpu.VMEM((CHUNKS, docs, part), jnp.bfloat16),
            pltpu.VMEM((SUBLANES, LANES), jnp.float32),
            pltpu.VMEM((mods, SUBLANES, LANES), jnp.float32),
            pltpu.VMEM((SUBLANES, LANES), jnp.float32),
            dma(()), dma((6,)), pltpu.SemaphoreType.REGULAR,
            dma(()), dma((chips,)),
            dma(()), dma((CHUNKS, chips - 1)), dma((CHUNKS,)),
            dma(()), dma(()), dma(()), dma(()),
        ],
        compiler_params=pltpu.CompilerParams(
            collective_id=0, has_side_effects=True, vmem_limit_bytes=48 * 1024 * 1024),
    )(*[pltpu.with_memory_space_constraint(x, pltpu.HBM) for x in (
        doc_ids.reshape(1, tokens), owners.reshape(1, docs), act[0], grad[0], pre_out[0], pre_in[0], train[0])])
    return scores[None]


def solution(mesh):
    blocks, mods = mesh.shape["blk"], mesh.shape["mod"]
    return jax.shard_map(
        functools.partial(body, blocks, mods),
        mesh=mesh,
        in_specs=(
            P("mod", None, "blk"),
            P("mod", None, "blk"),
            P("mod", "blk", None),
            P("mod", None, None),
            P("mod", None, None),
            P("blk", None),
            P(),
        ),
        out_specs=P("mod", None, "blk"),
        check_vma=False,
    )
```
